128 devices in a mesh: group: 2 (over y_lo), row: 8 (over x, y_hi), head: 8 (over z, core).
Axes of the slice: x: 4, y: 4 (y_hi: 2, y_lo: 2; y = y_hi * 2 + y_lo), z: 4, core: 2. Of those that a mesh axis runs over, the one named last changes fastest.
Arguments:
- latent: bfloat16 [2048, 3072], P('row', 'head'), may hold values from -6 to 6
- hint: bfloat16 [2048, 3072], P('row', 'head'), may hold values from -6 to 6
- timestep: int32 [1], replicated, may hold values from 0 to 7
- modulation: float32 [2, 8, 3, 3072], P('group'), may hold values from -3 to 3
- qkv_weight: bfloat16 [2, 3, 3072, 3072], P('group', None, None, 'head'), may hold values from -0.109375 to 0.109375
- out_weight: bfloat16 [2, 3072, 3072], P('group', None, 'head'), may hold values from -0.109375 to 0.109375
- zero_weight: bfloat16 [3072, 3072], P(None, 'head'), may hold values from -0.109375 to 0.109375
- cotangent: bfloat16 [2048, 3072], P('row', 'head'), may hold values from -6 to 6
Outputs:
- mixed: bfloat16 [2048, 3072], P('row', 'head')
- latent_grad: float32 [8, 2, 128, 3072], P('row', 'group', None, 'head')
- hint_grad: float32 [8, 2, 128, 3072], P('row', 'group', None, 'head')
- qkv_grad: float32 [3072, 3, 3072], P(('group', 'row'), None, 'head')
- out_grad: float32 [3072, 3072], P(('group', 'row'), 'head')
- zero_grad: float32 [3072, 3072], P(('group', 'row'), 'head')
The draws below stay inside these ranges and needn't reach their ends.
All inputs are finite; a program needn't handle non-finite values.
Results may differ from the reference program's by a relative error of at most 0.015.
Values may be sent and summed in bfloat16 or wider, within the bound.
No kernel may reach another device: no remote copies, remote signals or barrier semaphores. Data moves between devices by JAX's collectives and lax.ppermute only.
A program may use at most 128 MiB of HBM per device.

```python
import jax
import jax.numpy as jnp
from jax import lax

D = 3072
HEADS = 24
HD = 128
TOK_DEV = 256
STEPS = 8
TOKENS = 2048
N_ROW = 8


def block_scale(stream_key, dims, shards, low, top_value):
    gain = 1.0
    for dim, shards_of in shards:
        heights = jax.random.uniform(jax.random.fold_in(jax.random.fold_in(stream_key, 6), dim), (shards_of,), jnp.float32, low / len(shards), top_value / len(shards))
        gain = gain * jnp.repeat(jnp.exp(heights), dims[dim] // shards_of).reshape((-1,) + (1,) * (len(dims) - 1 - dim))
    return gain


def gaussian(key, shape, scale, limit, shards=(), held_as=jnp.bfloat16):
    drawn = scale * jax.random.normal(key, shape, jnp.float32)
    if shards:
        drawn = drawn * block_scale(key, shape, shards, -0.22, 0.18)
    return jnp.clip(drawn, -limit, limit).astype(held_as)


def setup_inputs(seed: int = 0) -> dict:
    key_list = jax.random.split(jax.random.key(seed), 9)
    latent = gaussian(key_list[0], (TOKENS, D), 1.0, 6.0, ((0, 8), (1, 8)))
    hint = gaussian(key_list[1], (TOKENS, D), 1.0, 6.0, ((0, 8), (1, 8)))
    timestep = jax.random.randint(key_list[2], (1,), 0, STEPS).astype(jnp.int32)
    modulation = gaussian(key_list[3], (2, STEPS, 3, D), 0.5, 3.0, ((0, 2),), jnp.float32)
    qkv_weight = gaussian(key_list[4], (2, 3, D, D), D ** -0.5, 0.109375, ((0, 2), (3, 8)))
    out_weight = gaussian(key_list[5], (2, D, D), D ** -0.5, 0.109375, ((0, 2), (2, 8)))
    zero_weight = gaussian(key_list[6], (D, D), D ** -0.5, 0.109375, ((1, 8),))
    cotangent = gaussian(key_list[7], (TOKENS, D), 1.0, 6.0, ((0, 8), (1, 8)))
    return dict(latent=latent, hint=hint, timestep=timestep, modulation=modulation, qkv_weight=qkv_weight, out_weight=out_weight, zero_weight=zero_weight, cotangent=cotangent)


EPS = 1e-06

def normalize(u, shift, scale):
    uf = u.astype(jnp.float32)
    mean = lax.optimization_barrier(jnp.mean(uf, axis=-1, keepdims=True))
    centred = uf - mean
    var = lax.optimization_barrier(jnp.mean(centred * centred, axis=-1, keepdims=True))
    rstd = lax.rsqrt(var + EPS)
    nhat = centred * rstd
    normed = (nhat * (1.0 + scale) + shift).astype(jnp.bfloat16)
    return (normed, nhat, rstd)

def split_heads(x):
    return x.reshape(TOKENS, HEADS, HD).transpose(1, 0, 2)

def merge_heads(x):
    return x.transpose(1, 0, 2).reshape(TOKENS, HEADS * HD)

def head_forward(args):
    qh, kh, vh = args
    scores = jnp.dot(qh, kh.T, preferred_element_type=jnp.float32) * HD ** (-0.5)
    top = lax.optimization_barrier(jnp.max(scores, axis=-1, keepdims=True))
    weights = jnp.exp(scores - top)
    total = lax.optimization_barrier(jnp.sum(weights, axis=-1, keepdims=True))
    out = jnp.dot(weights.astype(jnp.bfloat16), vh, preferred_element_type=jnp.float32) / total
    return (out, top[:, 0] + jnp.log(total[:, 0]))

def head_backward(args):
    qh, kh, vh, gh, lse, dsum = args
    scores = jnp.dot(qh, kh.T, preferred_element_type=jnp.float32) * HD ** (-0.5)
    probs = jnp.exp(scores - lse[:, None])
    dval = jnp.dot(probs.astype(jnp.bfloat16).T, gh, preferred_element_type=jnp.float32)
    dprobs = jnp.dot(gh, vh.T, preferred_element_type=jnp.float32)
    dscores = (probs * (dprobs - dsum[:, None])).astype(jnp.bfloat16)
    dquery = jnp.dot(dscores, kh, preferred_element_type=jnp.float32) * HD ** (-0.5)
    dkey = jnp.dot(dscores.T, qh, preferred_element_type=jnp.float32) * HD ** (-0.5)
    return (dquery, dkey, dval)

def forward_block(u, mods, w_qkv, w_out):
    normed, nhat, rstd = normalize(u, mods[0], mods[1])
    query = jnp.dot(normed, w_qkv[0], preferred_element_type=jnp.float32).astype(jnp.bfloat16)
    keys = jnp.dot(normed, w_qkv[1], preferred_element_type=jnp.float32).astype(jnp.bfloat16)
    values = jnp.dot(normed, w_qkv[2], preferred_element_type=jnp.float32).astype(jnp.bfloat16)
    out_heads, lse = lax.map(head_forward, (split_heads(query), split_heads(keys), split_heads(values)))
    attn = merge_heads(out_heads).astype(jnp.bfloat16)
    branch = jnp.dot(attn, w_out.T, preferred_element_type=jnp.float32)
    state = (u.astype(jnp.float32) + mods[2] * branch).astype(jnp.bfloat16)
    return (normed, nhat, rstd, query, keys, values, attn, lse, state)

def backward_block(saved, incoming, mods, w_qkv, w_out):
    normed, nhat, rstd, query, keys, values, attn, lse, state = saved
    gated = (mods[2] * incoming.astype(jnp.float32)).astype(jnp.bfloat16)
    attn_grad = jnp.dot(gated, w_out, preferred_element_type=jnp.float32).astype(jnp.bfloat16)
    dsum = lax.optimization_barrier(jnp.sum((attn_grad.astype(jnp.float32) * attn.astype(jnp.float32)).reshape(TOKENS, HEADS, HD), axis=-1)).T
    dq, dk, dv = lax.map(head_backward, (split_heads(query), split_heads(keys), split_heads(values), split_heads(attn_grad), lse, dsum))
    grads = jnp.stack([merge_heads(dq).astype(jnp.bfloat16), merge_heads(dk).astype(jnp.bfloat16), merge_heads(dv).astype(jnp.bfloat16)])
    dnorm = jnp.zeros((TOKENS, D), jnp.float32)
    for index in range(3):
        dnorm = dnorm + jnp.dot(grads[index], w_qkv[index].T, preferred_element_type=jnp.float32)
    scaled = dnorm * (1.0 + mods[1])
    first = lax.optimization_barrier(jnp.mean(scaled, axis=-1, keepdims=True))
    second = lax.optimization_barrier(jnp.mean(scaled * nhat, axis=-1, keepdims=True))
    d_in = incoming.astype(jnp.float32) + rstd * (scaled - first - nhat * second)
    return (d_in, gated, grads)

def reference(latent, hint, timestep, modulation, qkv_weight, out_weight, zero_weight, cotangent):
    pick = (jnp.arange(STEPS, dtype=jnp.int32) == timestep[0]).astype(jnp.float32)
    mods = lax.optimization_barrier(jnp.sum(modulation * pick[None, :, None, None], axis=1))
    first_in = (latent.astype(jnp.float32) + hint.astype(jnp.float32)).astype(jnp.bfloat16)
    control = forward_block(first_in, mods[0], qkv_weight[0], out_weight[0])
    main = forward_block(latent, mods[1], qkv_weight[1], out_weight[1])
    control_out = control[8]
    projected = jnp.dot(control_out, zero_weight.T, preferred_element_type=jnp.float32)
    mixed = (main[8].astype(jnp.float32) + projected).astype(jnp.bfloat16)
    hint_back = jnp.dot(cotangent, zero_weight, preferred_element_type=jnp.float32).astype(jnp.bfloat16)
    d_control, gated, grads = backward_block(control, hint_back, mods[0], qkv_weight[0], out_weight[0])
    d_main, unused_gated, unused_grads = backward_block(main, cotangent, mods[1], qkv_weight[1], out_weight[1])
    latent_grad = (d_control + d_main).reshape(N_ROW, 2, TOK_DEV // 2, D)
    hint_grad = d_control.reshape(N_ROW, 2, TOK_DEV // 2, D)
    qkv_grad = jnp.einsum('tc,pte->cpe', control[0].astype(jnp.float32), grads.astype(jnp.float32), precision=lax.Precision.HIGHEST)
    out_grad = jnp.einsum('tj,ti->ji', gated.astype(jnp.float32), control[6].astype(jnp.float32), precision=lax.Precision.HIGHEST)
    zero_grad = jnp.einsum('tj,ti->ji', cotangent.astype(jnp.float32), control_out.astype(jnp.float32), precision=lax.Precision.HIGHEST)
    return (mixed, latent_grad, hint_grad, qkv_grad, out_grad, zero_grad)
```

```python
import functools

import jax
import jax.numpy as jnp
from jax import lax
from jax.experimental import pallas as pl
from jax.experimental.pallas import tpu as pltpu
from jax.sharding import Mesh
from jax.sharding import PartitionSpec as P

HD = 128
ROW = ("row_0", "row_1")
HEAD = ("z", "core")
GROUP_ROW = ("group", "row_0", "row_1")
YAX = ("group", "row_1")
EPS = 1e-06
F32 = jnp.float32
BF16 = jnp.bfloat16


def dot_nn(a, b):
    return lax.dot_general(a, b, (((1,), (0,)), ((), ())), preferred_element_type=F32)


def dot_nt(a, b):
    return lax.dot_general(a, b, (((1,), (1,)), ((), ())), preferred_element_type=F32)


def swap(array, axis, size, distance):
    return lax.ppermute(array, axis, [(i, i ^ distance) for i in range(size)])


def cost(flops, moved, trans=0):
    return pl.CostEstimate(flops=flops, bytes_accessed=moved, transcendentals=trans)


def gather_head(own):
    mine = [own] + [swap(own, "z", 4, d) for d in (1, 2, 3)]
    theirs = [swap(a, "core", 2, 1) for a in mine]
    pieces = []
    for a, b in zip(mine, theirs):
        pieces += [a, b]
    return jnp.stack(pieces)


def sum_head(own, other):
    got = swap(other, "core", 2, 1)
    sums = [own[d].astype(F32) + got[d].astype(F32) for d in range(4)]
    total = sums[0]
    for d in (1, 2, 3):
        total = total + swap(sums[d].astype(BF16), "z", 4, d).astype(F32)
    return total


def norm_qkv_kernel(pos, u, mods, w, n_out, q_out, kv_out, stats, acc, mean_s, rstd_s):
    i = pl.program_id(0)
    chunks, _, width = u.shape
    full = chunks * width

    @pl.when(i == 0)
    def _():
        total = jnp.sum(u[0].astype(F32), axis=-1, keepdims=True)
        for p in range(1, chunks):
            total += jnp.sum(u[p].astype(F32), axis=-1, keepdims=True)
        mean = total / full
        square = jnp.zeros_like(mean)
        for p in range(chunks):
            c = u[p].astype(F32) - mean
            square += jnp.sum(c * c, axis=-1, keepdims=True)
        rstd = lax.rsqrt(square / full + EPS)
        mean_s[...] = mean
        rstd_s[...] = rstd
        stats[0] = jnp.broadcast_to(mean, stats.shape[1:])
        stats[1] = jnp.broadcast_to(rstd, stats.shape[1:])
        acc[...] = jnp.zeros_like(acc)

    nhat = (u[i].astype(F32) - mean_s[...]) * rstd_s[...]
    n = (nhat * (1.0 + mods[0, 1:2, :]) + mods[0, 0:1, :]).astype(BF16)
    n_out[0] = n
    for j in range(3):
        acc[:, j * width : (j + 1) * width] += dot_nn(n, w[j])

    @pl.when(i == chunks - 1)
    def _():
        q_out[...] = acc[:, :width].astype(BF16)
        kv_out[...] = acc[:, width:].astype(BF16)


def norm_qkv(pos, u, mods, w):
    chunks, tok, width = u.shape
    return pl.pallas_call(
        norm_qkv_kernel,
        grid_spec=pltpu.PrefetchScalarGridSpec(
            num_scalar_prefetch=1,
            grid=(chunks,),
            in_specs=[
                pl.BlockSpec((chunks, tok, width), lambda i, s: (0, 0, 0)),
                pl.BlockSpec((1, 8, width), lambda i, s: (s[i], 0, 0)),
                pl.BlockSpec((3, width, width), lambda i, s: (0, s[i], 0)),
            ],
            out_specs=[
                pl.BlockSpec((1, tok, width), lambda i, s: (i, 0, 0)),
                pl.BlockSpec((tok, width), lambda i, s: (0, 0)),
                pl.BlockSpec((tok, 2 * width), lambda i, s: (0, 0)),
                pl.BlockSpec((2, tok, 128), lambda i, s: (0, 0, 0)),
            ],
            scratch_shapes=[
                pltpu.VMEM((tok, 3 * width), F32),
                pltpu.VMEM((tok, 1), F32),
                pltpu.VMEM((tok, 1), F32),
            ],
        ),
        out_shape=[
            jax.ShapeDtypeStruct((chunks, tok, width), BF16),
            jax.ShapeDtypeStruct((tok, width), BF16),
            jax.ShapeDtypeStruct((tok, 2 * width), BF16),
            jax.ShapeDtypeStruct((2, tok, 128), F32),
        ],
        cost_estimate=cost(2 * tok * chunks * width * 3 * width, 12 * 2**20),
    )(pos, u, mods, w)


def contract_kernel(pos, x, w, out, acc):
    i = pl.program_id(0)
    part = dot_nn(x[0], w[...])

    @pl.when(i == 0)
    def _():
        acc[...] = part

    @pl.when(i > 0)
    def _():
        acc[...] += part

    @pl.when(i == pl.num_programs(0) - 1)
    def _():
        out[...] = acc[...].astype(BF16)


def contract(pos, x, w):
    chunks, tok, width = x.shape
    return pl.pallas_call(
        contract_kernel,
        grid_spec=pltpu.PrefetchScalarGridSpec(
            num_scalar_prefetch=1,
            grid=(chunks,),
            in_specs=[
                pl.BlockSpec((1, tok, width), lambda i, s: (i, 0, 0)),
                pl.BlockSpec((width, width), lambda i, s: (s[i], 0)),
            ],
            out_specs=pl.BlockSpec((tok, width), lambda i, s: (0, 0)),
            scratch_shapes=[pltpu.VMEM((tok, width), F32)],
        ),
        out_shape=jax.ShapeDtypeStruct((tok, width), BF16),
        cost_estimate=cost(2 * tok * chunks * width * width, 4 * 2**20),
    )(pos, x, w)


def spread_kernel(pos, a, w, own, other):
    i = pl.program_id(0)
    part = dot_nt(a[...], w[...]).astype(BF16)

    @pl.when(i < 4)
    def _():
        other[0] = part

    @pl.when(i >= 4)
    def _():
        own[0] = part


def spread_outs(tok, width):
    specs = [
        pl.BlockSpec((1, tok, width), lambda i, s: (jnp.maximum(i - 4, 0), 0, 0)),
        pl.BlockSpec((1, tok, width), lambda i, s: (jnp.minimum(i, 3), 0, 0)),
    ]
    return specs, [jax.ShapeDtypeStruct((4, tok, width), BF16)] * 2


def spread(pos, a, w):
    tok, width = a.shape
    specs, shapes = spread_outs(tok, width)
    return pl.pallas_call(
        spread_kernel,
        grid_spec=pltpu.PrefetchScalarGridSpec(
            num_scalar_prefetch=1,
            grid=(8,),
            in_specs=[
                pl.BlockSpec((tok, width), lambda i, s: (0, 0)),
                pl.BlockSpec((width, width), lambda i, s: (s[i], 0)),
            ],
            out_specs=specs,
        ),
        out_shape=shapes,
        cost_estimate=cost(2 * tok * 8 * width * width, 5 * 2**20),
    )(pos, a, w)


def spread_norm_kernel(pos, grads, w, u, mods, stats, own, other, sums, s1, s2):
    i = pl.program_id(0)
    part = dot_nt(grads[0], w[0]) + dot_nt(grads[1], w[1]) + dot_nt(grads[2], w[2])
    scaled = part * (1.0 + mods[0, 1:2, :])
    nhat = (u[0].astype(F32) - stats[0, :, :1]) * stats[1, :, :1]
    first = jnp.sum(scaled, axis=-1, keepdims=True)
    second = jnp.sum(scaled * nhat, axis=-1, keepdims=True)

    @pl.when(i == 0)
    def _():
        s1[...] = first
        s2[...] = second

    @pl.when(i > 0)
    def _():
        s1[...] += first
        s2[...] += second

    @pl.when(i < 4)
    def _():
        other[0] = part.astype(BF16)

    @pl.when(i >= 4)
    def _():
        own[0] = part.astype(BF16)

    @pl.when(i == 7)
    def _():
        tok = s1.shape[0]
        lane = lax.broadcasted_iota(jnp.int32, (tok, 128), 1)
        both = jnp.where(lane == 0, s1[...], jnp.where(lane == 1, s2[...], 0.0))
        sums[...] = jnp.transpose(both)[:8]


def spread_norm(pos, grads, w, u, mods, stats):
    _, tok, width = grads.shape
    specs, shapes = spread_outs(tok, width)
    return pl.pallas_call(
        spread_norm_kernel,
        grid_spec=pltpu.PrefetchScalarGridSpec(
            num_scalar_prefetch=1,
            grid=(8,),
            in_specs=[
                pl.BlockSpec((3, tok, width), lambda i, s: (0, 0, 0)),
                pl.BlockSpec((3, width, width), lambda i, s: (0, s[i], 0)),
                pl.BlockSpec((1, tok, width), lambda i, s: (2 * (i % 4) + 1 - i // 4, 0, 0)),
                pl.BlockSpec((1, 8, width), lambda i, s: (s[i], 0, 0)),
                pl.BlockSpec((2, tok, 128), lambda i, s: (0, 0, 0)),
            ],
            out_specs=specs + [pl.BlockSpec((8, tok), lambda i, s: (0, 0))],
            scratch_shapes=[pltpu.VMEM((tok, 1), F32), pltpu.VMEM((tok, 1), F32)],
        ),
        out_shape=shapes + [jax.ShapeDtypeStruct((8, tok), F32)],
        cost_estimate=cost(6 * tok * 8 * width * width, 12 * 2**20),
    )(pos, grads, w, u, mods, stats)


def attention_kernel(blocks, scaling, *refs):
    q_ref, g_ref = refs[:2]
    k_refs, v_refs = refs[2 : 2 + blocks], refs[2 + blocks : 2 + 2 * blocks]
    o_ref, dq_ref = refs[2 + 2 * blocks : 4 + 2 * blocks]
    dkv_refs = refs[4 + 2 * blocks : 4 + 3 * blocks]
    scores = refs[-1]
    q, g = q_ref[...], g_ref[...]
    tok = q.shape[0]
    peak = None
    for b in range(blocks):
        s = dot_nt(k_refs[b][...], q) * scaling
        scores[b] = s
        top = jnp.max(s, axis=0, keepdims=True)
        peak = top if peak is None else jnp.maximum(peak, top)
    total = jnp.zeros((1, tok), F32)
    acc = jnp.zeros((HD, tok), F32)
    for b in range(blocks):
        w = jnp.exp(scores[b] - peak)
        scores[b] = w
        total += jnp.sum(w, axis=0, keepdims=True)
        acc += dot_nn(jnp.transpose(v_refs[b][...]), w.astype(BF16))
    out_t = (acc / total).astype(BF16).astype(F32)
    o_ref[...] = jnp.transpose(out_t).astype(BF16)
    dsum = jnp.sum(jnp.transpose(g.astype(F32)) * out_t, axis=0, keepdims=True)
    inverse = 1.0 / total
    dq = jnp.zeros((HD, tok), F32)
    for b in range(blocks):
        probs = scores[b] * inverse
        dprobs = dot_nt(v_refs[b][...], g)
        ds = (probs * (dprobs - dsum)).astype(BF16)
        dkv_refs[b][0] = (dot_nn(ds, q) * scaling).astype(BF16)
        dkv_refs[b][1] = dot_nn(probs.astype(BF16), g).astype(BF16)
        dq += dot_nn(jnp.transpose(k_refs[b][...]), ds)
    dq_ref[...] = (jnp.transpose(dq) * scaling).astype(BF16)


def attention(query, grad, kv_blocks):
    tok, width = query.shape
    heads = width // HD
    blocks = len(kv_blocks)
    one = pl.BlockSpec((tok, HD), lambda j: (0, j))
    value = pl.BlockSpec((tok, HD), lambda j: (0, heads + j))
    both = pl.BlockSpec((2, tok, HD), lambda j: (0, 0, j))
    return pl.pallas_call(
        functools.partial(attention_kernel, blocks, HD**-0.5),
        grid=(heads,),
        in_specs=[one, one] + [one] * blocks + [value] * blocks,
        out_specs=[one, one] + [both] * blocks,
        out_shape=[jax.ShapeDtypeStruct((tok, width), BF16)] * 2
        + [jax.ShapeDtypeStruct((2, tok, width), BF16)] * blocks,
        scratch_shapes=[pltpu.VMEM((blocks, tok, tok), F32)],
        cost_estimate=cost(
            12 * tok * blocks * tok * width, 8 * 2**20, tok * blocks * tok * heads
        ),
    )(query, grad, *kv_blocks, *kv_blocks)


def token_sum_kernel(terms, place, own, other, *refs):
    xs, out, turned = refs[:terms], refs[terms], refs[terms + 1]
    i, c = pl.program_id(0), pl.program_id(1)
    tok = own.shape[1]

    @pl.when((c == 0) & (i == 0))
    def _():
        for d in range(terms):
            turned[:, d * tok : (d + 1) * tok] = jnp.transpose(own[d])

    @pl.when((c == 0) & (i == 1))
    def _():
        for d in range(terms):
            turned[:, d * tok : (d + 1) * tok] = jnp.transpose(other[d])

    acc = dot_nn(turned[:, :tok], xs[0][0])
    for d in range(1, terms):
        acc += dot_nn(turned[:, d * tok : (d + 1) * tok], xs[d][0])
    acc = acc.astype(BF16)
    half = acc.shape[0] // 2

    @pl.when(place[1] == 0)
    def _():
        out[0, 0, 0] = acc[:half]
        out[0, 1, 0] = acc[half:]

    @pl.when(place[1] == 1)
    def _():
        out[0, 0, 0] = acc[half:]
        out[0, 1, 0] = acc[:half]


def token_sum(place, own, other, xs):
    terms, tok, cols = own.shape
    kinds, _, width = xs[0].shape
    whole = pl.BlockSpec((terms, tok, cols), lambda i, c, s: (0, 0, 0))
    return pl.pallas_call(
        functools.partial(token_sum_kernel, terms),
        grid_spec=pltpu.PrefetchScalarGridSpec(
            num_scalar_prefetch=1,
            grid=(2, kinds),
            in_specs=[whole, whole]
            + [pl.BlockSpec((1, tok, width), lambda i, c, s: (c, 0, 0))] * terms,
            out_specs=pl.BlockSpec(
                (1, 2, 1, cols // 2, width), lambda i, c, s: (i ^ s[0], 0, c, 0, 0)
            ),
            scratch_shapes=[pltpu.VMEM((cols, terms * tok), BF16)],
        ),
        out_shape=jax.ShapeDtypeStruct((2, 2, kinds, cols // 2, width), BF16),
        cost_estimate=cost(4 * terms * tok * cols * kinds * width, 6 * 2**20),
    )(place, own, other, *xs)


def columns_along_x(source, head_pos, x_pos, core_pos):
    pieces = []
    for d in range(4):
        chunk = core_pos * 4 + (x_pos ^ d)
        piece = lax.dynamic_index_in_dim(source, head_pos ^ chunk, 0, keepdims=False)
        pieces.append(swap(piece, "row_0", 4, d) if d else piece)
    own = jnp.stack(pieces)
    return own, swap(own, "core", 2, 1)


def along_x(array):
    return [array] + [swap(array, "row_0", 4, d) for d in (1, 2, 3)]


def on_device(latent, hint, timestep, modulation, qkv_weight, out_weight, zero_weight, cotangent):
    tok, width = latent.shape
    x_pos, y_pos = lax.axis_index("row_0"), lax.axis_index("row_1")
    core_pos, group_pos = lax.axis_index("core"), lax.axis_index("group")
    head_pos = lax.axis_index("z") * 2 + core_pos
    control = group_pos == 0
    pos = head_pos ^ jnp.arange(8, dtype=jnp.int32)
    spread_pos = head_pos ^ jnp.array([1, 3, 5, 7, 0, 2, 4, 6], jnp.int32)
    place = jnp.stack([core_pos ^ group_pos, y_pos]).astype(jnp.int32)
    w_qkv, w_out = qkv_weight[0], out_weight[0]
    full_width = w_out.shape[0]

    chosen = lax.dynamic_index_in_dim(modulation[0], timestep[0], 0, keepdims=False)
    mods = jnp.pad(chosen.reshape(3, 8, width).transpose(1, 0, 2), ((0, 0), (0, 5), (0, 0)))
    mods_dev = lax.dynamic_index_in_dim(mods, head_pos, 0, keepdims=False)
    scale_dev, gate_dev = mods_dev[1], mods_dev[2]

    summed = (latent.astype(F32) + hint.astype(F32)).astype(BF16)
    inputs = jnp.where(control, summed, latent)
    whole = gather_head(inputs)
    cot_full = gather_head(cotangent)
    normed, query, kv, stats = norm_qkv(pos, whole, mods, w_qkv)
    kv_blocks = [kv] + [swap(kv, ROW, 8, d) for d in range(1, 8)]

    hint_back = contract(pos, cot_full, zero_weight)
    incoming = jnp.where(control, hint_back, cotangent)
    gated = (gate_dev * incoming.astype(F32)).astype(BF16)
    gated_full = gather_head(gated)
    attn_grad = contract(pos, gated_full, w_out)

    attn, dquery, *dkv = attention(query, attn_grad, kv_blocks)

    dkv_sum = dkv[0].astype(F32)
    for d in range(1, 8):
        dkv_sum = dkv_sum + swap(dkv[d], ROW, 8, d).astype(F32)
    grads = jnp.concatenate([dquery[None], dkv_sum.astype(BF16)])

    branch = sum_head(*spread(spread_pos, attn, w_out))
    state = (inputs.astype(F32) + gate_dev * branch).astype(BF16)
    other_state = swap(state, "group", 2, 1)
    control_out = jnp.where(control, state, other_state)
    main_out = jnp.where(control, other_state, state)
    projected = sum_head(*spread(spread_pos, control_out, zero_weight))
    mixed = (main_out.astype(F32) + projected).astype(BF16)

    own_terms, other_terms, sums = spread_norm(
        spread_pos, grads, w_qkv, whole, mods, stats
    )
    for axis, size, d in (("core", 2, 1), ("z", 4, 1), ("z", 4, 2)):
        sums = sums + swap(sums, axis, size, d)
    dnorm = sum_head(own_terms, other_terms)
    mean, rstd = stats[0, :, :1], stats[1, :, :1]
    nhat_dev = (inputs.astype(F32) - mean) * rstd
    first = sums[0][:, None] / full_width
    second = sums[1][:, None] / full_width
    d_in = incoming.astype(F32) + rstd * (dnorm * (1.0 + scale_dev) - first - nhat_dev * second)
    half = tok // 2
    own_half = lax.dynamic_slice_in_dim(d_in, group_pos * half, half, 0)
    sent_half = lax.dynamic_slice_in_dim(d_in, (1 - group_pos) * half, half, 0)
    other_half = swap(sent_half, "group", 2, 1)
    latent_grad = (own_half + other_half)[None, None]
    hint_grad = jnp.where(control, own_half, other_half)[None, None]

    normed_cols = columns_along_x(normed, head_pos, x_pos, core_pos)
    gated_or_cot = jnp.where(control, gated_full, cot_full)
    side_cols = columns_along_x(gated_or_cot, head_pos, x_pos, core_pos)
    attn_or_state = jnp.where(control, attn, control_out)
    side = token_sum(place, *side_cols, along_x(attn_or_state[None]))
    near = side[0, 0, 0].astype(F32) + swap(side[0, 1, 0], "row_1", 2, 1).astype(F32)
    far = swap(side[1, 0, 0], "group", 2, 1).astype(F32) + lax.ppermute(
        side[1, 1, 0], YAX, [(0, 3), (1, 2), (2, 1), (3, 0)]
    ).astype(F32)
    out_grad = jnp.where(control, near, far)
    zero_grad = jnp.where(control, far, near)

    main = token_sum(place, *normed_cols, along_x(grads))
    near = main[0, 0].astype(F32) + lax.ppermute(main[0, 1], YAX, [(0, 1), (1, 0)]).astype(F32)
    far = lax.ppermute(main[1, 0], YAX, [(0, 2), (1, 3)]).astype(F32) + lax.ppermute(
        main[1, 1], YAX, [(0, 3), (1, 2)]
    ).astype(F32)
    qkv_grad = jnp.where(control, near, far).transpose(1, 0, 2)
    return (mixed, latent_grad, hint_grad, qkv_grad, out_grad, zero_grad)


def solution(mesh):
    torus = Mesh(
        mesh.devices.reshape(mesh.shape["group"], 4, 2, 4, 2),
        ("group", "row_0", "row_1", "z", "core"),
    )
    return jax.shard_map(
        on_device,
        mesh=torus,
        in_specs=(
            P(ROW, HEAD),
            P(ROW, HEAD),
            P(),
            P("group", None, None, None),
            P("group", None, None, HEAD),
            P("group", None, HEAD),
            P(None, HEAD),
            P(ROW, HEAD),
        ),
        out_specs=(
            P(ROW, HEAD),
            P(ROW, "group", None, HEAD),
            P(ROW, "group", None, HEAD),
            P(GROUP_ROW, None, HEAD),
            P(GROUP_ROW, HEAD),
            P(GROUP_ROW, HEAD),
        ),
        check_vma=False,
    )
```

```python
import functools

import jax
import jax.numpy as jnp
from jax import lax
from jax.experimental import pallas as pl
from jax.experimental.pallas import tpu as pltpu
from jax.sharding import Mesh
from jax.sharding import PartitionSpec as P


HD = 128
ROW = ("row_0", "row_1")
HEAD = ("z", "core")
GROUP_ROW = ("group", "row_0", "row_1")
YAX = ("group", "row_1")
EPS = 1e-06
F32 = jnp.float32
BF16 = jnp.bfloat16
ANY = pl.BlockSpec(memory_space=pl.ANY)


def dot_nn(a, b):
    return lax.dot_general(a, b, (((1,), (0,)), ((), ())), preferred_element_type=F32)


def dot_nt(a, b):
    return lax.dot_general(a, b, (((1,), (1,)), ((), ())), preferred_element_type=F32)


def moved(array, axis, pairs):
    return lax.ppermute(array, axis, pairs)


def swap(array, axis, size, distance):
    return moved(array, axis, [(i, i ^ distance) for i in range(size)])


def cost(flops, size, trans=0):
    return pl.CostEstimate(flops=flops, bytes_accessed=size, transcendentals=trans)


def shaped(shape, dtype=BF16):
    return jax.ShapeDtypeStruct(shape, dtype)


def full(shape):
    return pl.BlockSpec(shape, lambda *a: (0,) * len(shape))


def run(body, place, args, specs, outs, scratch, estimate):
    return pl.pallas_call(
        body,
        grid_spec=pltpu.PrefetchScalarGridSpec(
            num_scalar_prefetch=1,
            grid=(1,),
            in_specs=specs,
            out_specs=[full(o.shape) for o in outs],
            scratch_shapes=scratch,
        ),
        out_shape=outs,
        cost_estimate=estimate,
    )(place, *args)


def gather_head(own):
    mine = [own] + [swap(own, "z", 4, d) for d in (1, 2, 3)]
    pieces = []
    for a in mine:
        pieces += [a, swap(a, "core", 2, 1)]
    return pieces


def sum_head(own, other):
    got = swap(other, "core", 2, 1)
    sums = [own[d].astype(F32) + got[d].astype(F32) for d in range(4)]
    total = sums[0]
    for d in (1, 2, 3):
        total = total + swap(sums[d].astype(BF16), "z", 4, d).astype(F32)
    return total


def lanes(index, width):
    return pl.ds(pl.multiple_of(index * width, 128), width)


def lay_out(place, pieces, whole):
    width = pieces[0].shape[1]
    for p, piece in enumerate(pieces):
        whole[:, lanes(place[0] ^ p, width)] = piece[...]


def norm_qkv_kernel(place, *refs):
    pieces, (mods, w) = refs[:8], refs[8:10]
    cols, q_out, kv_out, stats = refs[10:14]
    whole, wbuf, sems = refs[14:]
    width = pieces[0].shape[1]
    pair = 2 * width
    copies = []
    for c in range(3):
        copies.append(pltpu.make_async_copy(w.at[c], wbuf.at[c], sems.at[c]))
        copies[-1].start()
    lay_out(place, pieces, whole)
    features = 8 * width
    total = jnp.sum(pieces[0][...].astype(F32), axis=-1, keepdims=True)
    for p in range(1, 8):
        total += jnp.sum(pieces[p][...].astype(F32), axis=-1, keepdims=True)
    mean = total / features
    square = jnp.zeros_like(mean)
    for p in range(8):
        c = pieces[p][...].astype(F32) - mean
        square += jnp.sum(c * c, axis=-1, keepdims=True)
    rstd = lax.rsqrt(square / features + EPS)
    stats[0] = jnp.broadcast_to(mean, stats.shape[1:])
    stats[1] = jnp.broadcast_to(rstd, stats.shape[1:])
    for k in range(8):
        at = slice(k * width, (k + 1) * width)
        nhat = (whole[:, at].astype(F32) - mean) * rstd
        n = (nhat * (1.0 + mods[1:2, at]) + mods[0:1, at]).astype(BF16)
        whole[:, at] = n

        @pl.when(place[1] == k // 4)
        def _():
            cols[place[2] ^ (k % 4)] = n

    outs = (q_out.at[:, :], kv_out.at[:, :width], kv_out.at[:, width:pair])
    for c in range(3):
        copies[c].wait()
        outs[c][...] = dot_nn(whole[...], wbuf[c]).astype(BF16)


def norm_qkv(place, pieces, mods, w):
    tok, width = pieces[0].shape
    return run(
        norm_qkv_kernel,
        place,
        (*pieces, mods, w),
        [full((tok, width))] * 8 + [full(mods.shape), ANY],
        [
            shaped((4, tok, width)),
            shaped((tok, width)),
            shaped((tok, 2 * width)),
            shaped((2, tok, 128), F32),
        ],
        [
            pltpu.VMEM((tok, 8 * width), BF16),
            pltpu.VMEM(w.shape, BF16),
            pltpu.SemaphoreType.DMA((3,)),
        ],
        cost(2 * tok * 8 * width * 3 * width, 12 * 2**20),
    )


def hint_kernel(place, *refs):
    pieces, (mods, w) = refs[:8], refs[8:10]
    incoming, gated, cols = refs[10:13]
    whole, wbuf, sem = refs[13:]
    width = pieces[0].shape[1]
    copy = pltpu.make_async_copy(w, wbuf, sem.at[0])
    copy.start()
    lay_out(place, pieces, whole)
    for d in range(4):
        cols[d] = whole[:, lanes(place[1] * 4 + (place[2] ^ d), width)]
    copy.wait()
    back = dot_nn(whole[...], wbuf[...]).astype(BF16)
    got = jnp.where(place[3] == 0, back, pieces[0][...])
    incoming[...] = got
    gate = mods[2:3, lanes(place[0], width)]
    gated[...] = (gate * got.astype(F32)).astype(BF16)


def hint_back(place, pieces, mods, w):
    tok, width = pieces[0].shape
    return run(
        hint_kernel,
        place,
        (*pieces, mods, w),
        [full((tok, width))] * 8 + [full(mods.shape), ANY],
        [shaped((tok, width)), shaped((tok, width)), shaped((4, tok, width))],
        [
            pltpu.VMEM((tok, 8 * width), BF16),
            pltpu.VMEM(w.shape, BF16),
            pltpu.SemaphoreType.DMA((1,)),
        ],
        cost(2 * tok * 8 * width * width, 6 * 2**20),
    )


def branch_grad_kernel(place, *refs):
    pieces, (w, ncols, ccols) = refs[:8], refs[8:11]
    out, packs = refs[11], refs[12:16]
    whole, wbuf, sem = refs[16:]
    width = pieces[0].shape[1]
    copy = pltpu.make_async_copy(w, wbuf, sem.at[0])
    copy.start()
    lay_out(place, pieces, whole)
    for d in range(4):
        packs[d][0] = ncols[d]

        @pl.when(place[3] == 0)
        def _():
            packs[d][1] = whole[:, lanes(place[1] * 4 + (place[2] ^ d), width)]

        @pl.when(place[3] != 0)
        def _():
            packs[d][1] = ccols[d]

    copy.wait()
    out[...] = dot_nn(whole[...], wbuf[...]).astype(BF16)


def branch_grad(place, pieces, w, ncols, ccols):
    tok, width = pieces[0].shape
    return run(
        branch_grad_kernel,
        place,
        (*pieces, w, ncols, ccols),
        [full((tok, width))] * 8 + [ANY, full(ncols.shape), full(ccols.shape)],
        [shaped((tok, width))] + [shaped((2, tok, width))] * 4,
        [
            pltpu.VMEM((tok, 8 * width), BF16),
            pltpu.VMEM(w.shape, BF16),
            pltpu.SemaphoreType.DMA((1,)),
        ],
        cost(2 * tok * 8 * width * width, 8 * 2**20),
    )


def spread_kernel(place, a, w, own, other, wbuf, sems):
    width = a.shape[1]
    pair = 2 * width
    copies = []
    for d in range(4):
        rows = pl.ds(pl.multiple_of(((place[0] // 2) ^ d) * pair, pair), pair)
        copies.append(pltpu.make_async_copy(w.at[rows], wbuf.at[d], sems.at[d]))
        copies[-1].start()
    for d in range(4):
        copies[d].wait()
        part = dot_nt(a[...], wbuf[d]).astype(BF16)

        @pl.when(place[1] == 0)
        def _():
            own[d] = part[:, :width]
            other[d] = part[:, width:]

        @pl.when(place[1] != 0)
        def _():
            own[d] = part[:, width:]
            other[d] = part[:, :width]


def spread(place, a, w):
    tok, width = a.shape
    return run(
        spread_kernel,
        place,
        (a, w),
        [full((tok, width)), ANY],
        [shaped((4, tok, width))] * 2,
        [pltpu.VMEM((4, 2 * width, width), BF16), pltpu.SemaphoreType.DMA((4,))],
        cost(2 * tok * 8 * width * width, 6 * 2**20),
    )


def spread_norm_kernel(place, grads, w, mods, stats, *refs):
    pieces, (own, other, sums, wbuf, sems) = refs[:8], refs[8:]
    tok, width = pieces[0].shape
    pair = 2 * width
    copies = []
    for d in range(4):
        rows = pl.ds(pl.multiple_of(((place[0] // 2) ^ d) * pair, pair), pair)
        copies.append(pltpu.make_async_copy(w.at[:, rows], wbuf.at[d], sems.at[d]))
        copies[-1].start()
    mean, rstd = stats[0, :, :1], stats[1, :, :1]
    first = jnp.zeros((tok, 1), F32)
    second = jnp.zeros((tok, 1), F32)
    for d in range(4):
        copies[d].wait()
        part = (
            dot_nt(grads[0], wbuf[d, 0])
            + dot_nt(grads[1], wbuf[d, 1])
            + dot_nt(grads[2], wbuf[d, 2])
        )
        low, high = part[:, :width], part[:, width:]
        halves = (
            jnp.where(place[1] == 0, low, high),
            jnp.where(place[1] == 0, high, low),
        )
        for cc, (share, out) in enumerate(zip(halves, (own, other))):
            out[d] = share.astype(BF16)
            scale = 1.0 + mods[1:2, lanes(place[0] ^ (2 * d + cc), width)]
            scaled = share * scale
            nhat = (pieces[2 * d + cc][...].astype(F32) - mean) * rstd
            first += jnp.sum(scaled, axis=-1, keepdims=True)
            second += jnp.sum(scaled * nhat, axis=-1, keepdims=True)
    lane = lax.broadcasted_iota(jnp.int32, (tok, 128), 1)
    both = jnp.where(lane == 0, first, jnp.where(lane == 1, second, 0.0))
    sums[...] = jnp.transpose(both)[:8]


def spread_norm(place, grads, w, mods, stats, pieces):
    _, tok, width = grads.shape
    return run(
        spread_norm_kernel,
        place,
        (grads, w, mods, stats, *pieces),
        [full(grads.shape), ANY, full(mods.shape), full(stats.shape)]
        + [full((tok, width))] * 8,
        [shaped((4, tok, width))] * 2 + [shaped((8, tok), F32)],
        [pltpu.VMEM((4, 3, 2 * width, width), BF16), pltpu.SemaphoreType.DMA((4,))],
        cost(6 * tok * 8 * width * width, 14 * 2**20),
    )


def attention_kernel(scaling, q_ref, g_ref, k_ref, v_ref, o_ref, dq_ref, dkv_ref, scores):
    q, g = q_ref[...], g_ref[...]
    blocks, tok = k_ref.shape[:2]
    peak = None
    for b in range(blocks):
        s = dot_nt(k_ref[b], q) * scaling
        scores[b] = s
        top = jnp.max(s, axis=0, keepdims=True)
        peak = top if peak is None else jnp.maximum(peak, top)
    total = jnp.zeros((1, tok), F32)
    acc = jnp.zeros((HD, tok), F32)
    for b in range(blocks):
        w = jnp.exp(scores[b] - peak)
        scores[b] = w
        total += jnp.sum(w, axis=0, keepdims=True)
        acc += dot_nn(jnp.transpose(v_ref[b]), w.astype(BF16))
    out_t = (acc / total).astype(BF16).astype(F32)
    o_ref[...] = jnp.transpose(out_t).astype(BF16)
    dsum = jnp.sum(jnp.transpose(g.astype(F32)) * out_t, axis=0, keepdims=True)
    inverse = 1.0 / total
    dq = jnp.zeros((HD, tok), F32)
    for b in range(blocks):
        probs = scores[b] * inverse
        dprobs = dot_nt(v_ref[b], g)
        ds = (probs * (dprobs - dsum)).astype(BF16)
        dkv_ref[b, 0] = (dot_nn(ds, q) * scaling).astype(BF16)
        dkv_ref[b, 1] = dot_nn(probs.astype(BF16), g).astype(BF16)
        dq += dot_nn(jnp.transpose(k_ref[b]), ds)
    dq_ref[...] = (jnp.transpose(dq) * scaling).astype(BF16)


def attention(query, grad, kv):
    tok, width = query.shape
    heads, blocks = width // HD, kv.shape[0]
    one = pl.BlockSpec((tok, HD), lambda j: (0, j))
    return pl.pallas_call(
        functools.partial(attention_kernel, HD**-0.5),
        grid=(heads,),
        in_specs=[
            one,
            one,
            pl.BlockSpec((blocks, tok, HD), lambda j: (0, 0, j)),
            pl.BlockSpec((blocks, tok, HD), lambda j: (0, 0, heads + j)),
        ],
        out_specs=[one, one, pl.BlockSpec((blocks, 2, tok, HD), lambda j: (0, 0, 0, j))],
        out_shape=[
            shaped((tok, width)),
            shaped((tok, width)),
            shaped((blocks, 2, tok, width)),
        ],
        scratch_shapes=[pltpu.VMEM((blocks, tok, tok), F32)],
        cost_estimate=cost(12 * tok * blocks * tok * width, 8 * 2**20, tok * blocks * tok * heads),
    )(query, grad, kv, kv)


def token_sum_kernel(place, *refs):
    own, other, xs, out, turned = refs[:4], refs[4:8], refs[8:12], refs[12], refs[13]
    i, c = pl.program_id(0), pl.program_id(1)
    tok = own[0].shape[1]

    for half, cols in enumerate((own, other)):

        @pl.when((c == 0) & (i == half))
        def _():
            for d in range(4):
                turned[:, d * tok : (d + 1) * tok] = jnp.transpose(cols[d][0])

    acc = dot_nn(turned[:, :tok], xs[0][0])
    for d in range(1, 4):
        acc += dot_nn(turned[:, d * tok : (d + 1) * tok], xs[d][0])
    acc = acc.astype(BF16)
    half = acc.shape[0] // 2

    @pl.when(place[5] == 0)
    def _():
        out[0, 0, 0] = acc[:half]
        out[0, 1, 0] = acc[half:]

    @pl.when(place[5] != 0)
    def _():
        out[0, 0, 0] = acc[half:]
        out[0, 1, 0] = acc[:half]


def token_sum(place, which, own, other, xs):
    _, tok, cols = own[0].shape
    kinds, _, width = xs[0].shape
    column = pl.BlockSpec((1, tok, cols), lambda i, c, s: (which, 0, 0))
    return pl.pallas_call(
        token_sum_kernel,
        grid_spec=pltpu.PrefetchScalarGridSpec(
            num_scalar_prefetch=1,
            grid=(2, kinds),
            in_specs=[column] * 8
            + [pl.BlockSpec((1, tok, width), lambda i, c, s: (c, 0, 0))] * 4,
            out_specs=pl.BlockSpec(
                (1, 2, 1, cols // 2, width), lambda i, c, s: (i ^ s[4], 0, c, 0, 0)
            ),
            scratch_shapes=[pltpu.VMEM((cols, 4 * tok), BF16)],
        ),
        out_shape=shaped((2, 2, kinds, cols // 2, width)),
        cost_estimate=cost(16 * tok * cols * kinds * width, 6 * 2**20),
    )(place, *own, *other, *xs)


def along_x(array):
    return [array] + [swap(array, "row_0", 4, d) for d in (1, 2, 3)]


def on_device(latent, hint, timestep, modulation, qkv_weight, out_weight, zero_weight, cotangent):
    tok, width = latent.shape
    x_pos, y_pos = lax.axis_index("row_0"), lax.axis_index("row_1")
    core_pos, group_pos = lax.axis_index("core"), lax.axis_index("group")
    head_pos = lax.axis_index("z") * 2 + core_pos
    control = group_pos == 0
    place = jnp.stack(
        [head_pos, core_pos, x_pos, group_pos, core_pos ^ group_pos, y_pos]
    ).astype(jnp.int32)
    w_qkv, w_out = qkv_weight[0], out_weight[0]
    full_width = w_out.shape[0]

    chosen = lax.dynamic_index_in_dim(modulation[0], timestep[0], 0, keepdims=False)
    mods_dev = lax.dynamic_slice_in_dim(chosen, head_pos * width, width, 1)
    scale_dev, gate_dev = mods_dev[1], mods_dev[2]

    summed = (latent.astype(F32) + hint.astype(F32)).astype(BF16)
    inputs = jnp.where(control, summed, latent)
    whole = gather_head(inputs)
    cot_late = lax.optimization_barrier((cotangent, whole[2], whole[4], whole[6]))[0]
    cot_full = gather_head(cot_late)
    ncols, query, kv, stats = norm_qkv(place, whole, chosen, w_qkv)
    kv_full = lax.all_to_all(
        jnp.broadcast_to(kv, (8, *kv.shape)), ROW, split_axis=0, concat_axis=0, tiled=True
    )

    incoming, gated, ccols = hint_back(place, cot_full, chosen, zero_weight)
    gated_full = gather_head(gated)
    attn_grad, *packs = branch_grad(place, gated_full, w_out, ncols, ccols)
    cols = packs[:1] + [swap(packs[d], "row_0", 4, d) for d in (1, 2, 3)]
    cols_other = [swap(a, "core", 2, 1) for a in cols]

    attn, dquery, dkv = attention(query, attn_grad, kv_full)
    dkv_all = lax.all_to_all(dkv, ROW, split_axis=0, concat_axis=0, tiled=True)

    branch = sum_head(*spread(place, attn, w_out))
    state = (inputs.astype(F32) + gate_dev * branch).astype(BF16)
    other_state = swap(state, "group", 2, 1)
    control_out = jnp.where(control, state, other_state)
    main_out = jnp.where(control, other_state, state)
    zero_own, zero_other = spread(place, control_out, zero_weight)

    dkv_all, zero_own = lax.optimization_barrier((dkv_all, zero_own))
    dkv_sum = jnp.sum(dkv_all.astype(F32), axis=0).astype(BF16)
    grads = jnp.concatenate([dquery[None], dkv_sum])
    grads_x = along_x(grads)
    projected = sum_head(zero_own, zero_other)
    mixed = (main_out.astype(F32) + projected).astype(BF16)
    own_terms, other_terms, sums = spread_norm(place, grads, w_qkv, chosen, stats, whole)
    for axis, size, d in (("core", 2, 1), ("z", 4, 1), ("z", 4, 2)):
        sums = sums + swap(sums, axis, size, d)
    dnorm = sum_head(own_terms, other_terms)
    mean, rstd = stats[0, :, :1], stats[1, :, :1]
    nhat_dev = (inputs.astype(F32) - mean) * rstd
    first = sums[0][:, None] / full_width
    second = sums[1][:, None] / full_width
    d_in = incoming.astype(F32) + rstd * (dnorm * (1.0 + scale_dev) - first - nhat_dev * second)
    half = tok // 2
    own_half = lax.dynamic_slice_in_dim(d_in, group_pos * half, half, 0)
    sent_half = lax.dynamic_slice_in_dim(d_in, (1 - group_pos) * half, half, 0)
    other_half = swap(sent_half, "group", 2, 1)
    latent_grad = (own_half + other_half)[None, None]
    hint_grad = jnp.where(control, own_half, other_half)[None, None]

    attn_or_state = jnp.where(control, attn, control_out)
    side = token_sum(place, 1, cols, cols_other, along_x(attn_or_state[None]))
    near = side[0, 0, 0].astype(F32) + swap(side[0, 1, 0], "row_1", 2, 1).astype(F32)
    far = swap(side[1, 0, 0], "group", 2, 1).astype(F32) + moved(
        side[1, 1, 0], YAX, [(0, 3), (1, 2), (2, 1), (3, 0)]
    ).astype(F32)
    out_grad = jnp.where(control, near, far)
    zero_grad = jnp.where(control, far, near)

    main = token_sum(place, 0, cols, cols_other, grads_x)
    near = main[0, 0].astype(F32) + moved(main[0, 1], YAX, [(0, 1), (1, 0)]).astype(F32)
    far = moved(main[1, 0], YAX, [(0, 2), (1, 3)]).astype(F32) + moved(
        main[1, 1], YAX, [(0, 3), (1, 2)]
    ).astype(F32)
    qkv_grad = jnp.where(control, near, far).transpose(1, 0, 2)
    return (mixed, latent_grad, hint_grad, qkv_grad, out_grad, zero_grad)


def solution(mesh):
    torus = Mesh(
        mesh.devices.reshape(mesh.shape["group"], 4, 2, 4, 2),
        ("group", "row_0", "row_1", "z", "core"),
    )

    return jax.shard_map(
        on_device,
        mesh=torus,
        in_specs=(
            P(ROW, HEAD),
            P(ROW, HEAD),
            P(),
            P("group", None, None, None),
            P("group", None, None, HEAD),
            P("group", None, HEAD),
            P(None, HEAD),
            P(ROW, HEAD),
        ),
        out_specs=(
            P(ROW, HEAD),
            P(ROW, "group", None, HEAD),
            P(ROW, "group", None, HEAD),
            P(GROUP_ROW, None, HEAD),
            P(GROUP_ROW, HEAD),
            P(GROUP_ROW, HEAD),
        ),
        check_vma=False,
    )
```

```python
import functools

import jax
import jax.numpy as jnp
from jax import lax
from jax.experimental import pallas as pl
from jax.experimental.pallas import tpu as pltpu
from jax.sharding import Mesh
from jax.sharding import PartitionSpec as P


HD = 128
ROW = ("row_0", "row_1")
HEAD = ("z", "core")
GROUP_ROW = ("group", "row_0", "row_1")
YAX = ("group", "row_1")
EPS = 1e-06
F32 = jnp.float32
BF16 = jnp.bfloat16
ANY = pl.BlockSpec(memory_space=pl.ANY)


def dot_nn(a, b):
    return lax.dot_general(a, b, (((1,), (0,)), ((), ())), preferred_element_type=F32)


def dot_nt(a, b):
    return lax.dot_general(a, b, (((1,), (1,)), ((), ())), preferred_element_type=F32)


def moved(array, axis, pairs):
    return lax.ppermute(array, axis, pairs)


def swap(array, axis, size, distance):
    return moved(array, axis, [(i, i ^ distance) for i in range(size)])


def cost(flops, size, trans=0):
    return pl.CostEstimate(flops=flops, bytes_accessed=size, transcendentals=trans)


def shaped(shape, dtype=BF16):
    return jax.ShapeDtypeStruct(shape, dtype)


def full(shape):
    return pl.BlockSpec(shape, lambda *a: (0,) * len(shape))


def run(body, place, args, specs, outs, scratch, estimate):
    return pl.pallas_call(
        body,
        grid_spec=pltpu.PrefetchScalarGridSpec(
            num_scalar_prefetch=1,
            grid=(1,),
            in_specs=specs,
            out_specs=[full(o.shape) for o in outs],
            scratch_shapes=scratch,
        ),
        out_shape=outs,
        cost_estimate=estimate,
    )(place, *args)


def gather_head(own):
    mine = [own] + [swap(own, "z", 4, d) for d in (1, 2, 3)]
    pieces = []
    for a in mine:
        pieces += [a, swap(a, "core", 2, 1)]
    return pieces


def sum_head(own, other):
    got = swap(other, "core", 2, 1)
    sums = [own[d].astype(F32) + got[d].astype(F32) for d in range(4)]
    total = sums[0]
    for d in (1, 2, 3):
        total = total + swap(sums[d].astype(BF16), "z", 4, d).astype(F32)
    return total


def lanes(index, width):
    return pl.ds(pl.multiple_of(index * width, 128), width)


def lay_out(place, pieces, whole):
    width = pieces[0].shape[1]
    for p, piece in enumerate(pieces):
        whole[:, lanes(place[0] ^ p, width)] = piece[...]


def norm_qkv_kernel(place, *refs):
    pieces, (mods, w) = refs[:8], refs[8:10]
    cols, qkv, stats = refs[10:13]
    whole, wbuf, sems = refs[13:]
    tok, width = pieces[0].shape

    def fetch(c):
        return pltpu.make_async_copy(w.at[c], wbuf.at[c], sems.at[c])

    for c in range(3):
        fetch(c).start()
    lay_out(place, pieces, whole)
    features = 8 * width
    zero = jnp.zeros((tok, 1), F32)

    def chunk(k):
        return whole[:, lanes(k, width)].astype(F32)

    mean = lax.fori_loop(
        0, 8, lambda k, t: t + jnp.sum(chunk(k), axis=-1, keepdims=True), zero, unroll=2
    ) / features

    def squares(k, t):
        c = chunk(k) - mean
        return t + jnp.sum(c * c, axis=-1, keepdims=True)

    rstd = lax.rsqrt(lax.fori_loop(0, 8, squares, zero, unroll=2) / features + EPS)
    stats[0] = jnp.broadcast_to(mean, stats.shape[1:])
    stats[1] = jnp.broadcast_to(rstd, stats.shape[1:])

    @pl.loop(0, 8, unroll=2)
    def _(k):
        at = lanes(k, width)
        nhat = (chunk(k) - mean) * rstd
        n = (nhat * (1.0 + mods[1:2, at]) + mods[0:1, at]).astype(BF16)
        whole[:, at] = n

        @pl.when(place[1] == k // 4)
        def _():
            cols[place[2] ^ (k % 4)] = n

    @pl.loop(0, 3)
    def _(c):
        fetch(c).wait()
        qkv[c] = dot_nn(whole[...], wbuf[c]).astype(BF16)


def norm_qkv(place, pieces, mods, w):
    tok, width = pieces[0].shape
    return run(
        norm_qkv_kernel,
        place,
        (*pieces, mods, w),
        [full((tok, width))] * 8 + [full(mods.shape), ANY],
        [shaped((4, tok, width)), shaped((3, tok, width)), shaped((2, tok, 128), F32)],
        [
            pltpu.VMEM((tok, 8 * width), BF16),
            pltpu.VMEM(w.shape, BF16),
            pltpu.SemaphoreType.DMA((3,)),
        ],
        cost(2 * tok * 8 * width * 3 * width, 12 * 2**20),
    )


def hint_kernel(place, *refs):
    pieces, (mods, w) = refs[:8], refs[8:10]
    incoming, gated, cols = refs[10:13]
    whole, wbuf, sem = refs[13:]
    width = pieces[0].shape[1]
    copy = pltpu.make_async_copy(w, wbuf, sem.at[0])
    copy.start()
    lay_out(place, pieces, whole)
    for d in range(4):
        cols[d] = whole[:, lanes(place[1] * 4 + (place[2] ^ d), width)]
    copy.wait()
    back = dot_nn(whole[...], wbuf[...]).astype(BF16)
    got = jnp.where(place[3] == 0, back, pieces[0][...])
    incoming[...] = got
    gate = mods[2:3, lanes(place[0], width)]
    gated[...] = (gate * got.astype(F32)).astype(BF16)


def hint_back(place, pieces, mods, w):
    tok, width = pieces[0].shape
    return run(
        hint_kernel,
        place,
        (*pieces, mods, w),
        [full((tok, width))] * 8 + [full(mods.shape), ANY],
        [shaped((tok, width)), shaped((tok, width)), shaped((4, tok, width))],
        [
            pltpu.VMEM((tok, 8 * width), BF16),
            pltpu.VMEM(w.shape, BF16),
            pltpu.SemaphoreType.DMA((1,)),
        ],
        cost(2 * tok * 8 * width * width, 6 * 2**20),
    )


def branch_grad_kernel(place, *refs):
    pieces, (w, ncols, ccols) = refs[:8], refs[8:11]
    out, packs = refs[11], refs[12:16]
    whole, wbuf, sem = refs[16:]
    width = pieces[0].shape[1]
    copy = pltpu.make_async_copy(w, wbuf, sem.at[0])
    copy.start()
    lay_out(place, pieces, whole)
    for d in range(4):
        packs[d][0] = ncols[d]

        @pl.when(place[3] == 0)
        def _():
            packs[d][1] = whole[:, lanes(place[1] * 4 + (place[2] ^ d), width)]

        @pl.when(place[3] != 0)
        def _():
            packs[d][1] = ccols[d]

    copy.wait()
    out[...] = dot_nn(whole[...], wbuf[...]).astype(BF16)


def branch_grad(place, pieces, w, ncols, ccols):
    tok, width = pieces[0].shape
    return run(
        branch_grad_kernel,
        place,
        (*pieces, w, ncols, ccols),
        [full((tok, width))] * 8 + [ANY, full(ncols.shape), full(ccols.shape)],
        [shaped((tok, width))] + [shaped((2, tok, width))] * 4,
        [
            pltpu.VMEM((tok, 8 * width), BF16),
            pltpu.VMEM(w.shape, BF16),
            pltpu.SemaphoreType.DMA((1,)),
        ],
        cost(2 * tok * 8 * width * width, 8 * 2**20),
    )


def spread_kernel(place, a, w, own, other, wbuf, sems):
    width = a.shape[1]
    pair = 2 * width
    copies = []
    for d in range(4):
        rows = pl.ds(pl.multiple_of(((place[0] // 2) ^ d) * pair, pair), pair)
        copies.append(pltpu.make_async_copy(w.at[rows], wbuf.at[d], sems.at[d]))
        copies[-1].start()
    for d in range(4):
        copies[d].wait()
        part = dot_nt(a[...], wbuf[d]).astype(BF16)

        @pl.when(place[1] == 0)
        def _():
            own[d] = part[:, :width]
            other[d] = part[:, width:]

        @pl.when(place[1] != 0)
        def _():
            own[d] = part[:, width:]
            other[d] = part[:, :width]


def spread(place, a, w):
    tok, width = a.shape
    return run(
        spread_kernel,
        place,
        (a, w),
        [full((tok, width)), ANY],
        [shaped((4, tok, width))] * 2,
        [pltpu.VMEM((4, 2 * width, width), BF16), pltpu.SemaphoreType.DMA((4,))],
        cost(2 * tok * 8 * width * width, 6 * 2**20),
    )


def spread_norm_kernel(place, grads, w, mods, stats, *refs):
    pieces, (own, other, sums, whole, wbuf, sems) = refs[:8], refs[8:]
    tok, width = pieces[0].shape
    pair = 2 * width

    def fetch(d):
        rows = pl.ds(pl.multiple_of(((place[0] // 2) ^ d) * pair, pair), pair)
        return pltpu.make_async_copy(w.at[:, rows], wbuf.at[d], sems.at[d])

    for d in range(4):
        fetch(d).start()
    lay_out(place, pieces, whole)
    mean, rstd = stats[0, :, :1], stats[1, :, :1]
    zero = jnp.zeros((tok, 1), F32)

    def step(d, totals):
        first, second = totals
        fetch(d).wait()
        part = (
            dot_nt(grads[0], wbuf[d, 0])
            + dot_nt(grads[1], wbuf[d, 1])
            + dot_nt(grads[2], wbuf[d, 2])
        )
        low, high = part[:, :width].astype(BF16), part[:, width:].astype(BF16)

        @pl.when(place[1] == 0)
        def _():
            own[d] = low
            other[d] = high

        @pl.when(place[1] != 0)
        def _():
            own[d] = high
            other[d] = low

        at = lanes((place[0] // 2) ^ d, pair)
        scaled = part * (1.0 + mods[1:2, at])
        nhat = (whole[:, at].astype(F32) - mean) * rstd
        first += jnp.sum(scaled, axis=-1, keepdims=True)
        second += jnp.sum(scaled * nhat, axis=-1, keepdims=True)
        return first, second

    first, second = lax.fori_loop(0, 4, step, (zero, zero))
    lane = lax.broadcasted_iota(jnp.int32, (tok, 128), 1)
    both = jnp.where(lane == 0, first, jnp.where(lane == 1, second, 0.0))
    sums[...] = jnp.transpose(both)[:8]


def spread_norm(place, grads, w, mods, stats, pieces):
    _, tok, width = grads.shape
    return run(
        spread_norm_kernel,
        place,
        (grads, w, mods, stats, *pieces),
        [full(grads.shape), ANY, full(mods.shape), full(stats.shape)]
        + [full((tok, width))] * 8,
        [shaped((4, tok, width))] * 2 + [shaped((8, tok), F32)],
        [
            pltpu.VMEM((tok, 8 * width), BF16),
            pltpu.VMEM((4, 3, 2 * width, width), BF16),
            pltpu.SemaphoreType.DMA((4,)),
        ],
        cost(6 * tok * 8 * width * width, 14 * 2**20),
    )


def attention_kernel(scaling, q_ref, g_ref, k_ref, v_ref, o_ref, dq_ref, dkv_ref, scores):
    q, g = q_ref[0], g_ref[...]
    blocks, _, tok, _ = k_ref.shape
    peak = None
    for b in range(blocks):
        s = dot_nt(k_ref[b, 0], q) * scaling
        scores[b] = s
        top = jnp.max(s, axis=0, keepdims=True)
        peak = top if peak is None else jnp.maximum(peak, top)
    total = jnp.zeros((1, tok), F32)
    acc = jnp.zeros((HD, tok), F32)
    for b in range(blocks):
        w = jnp.exp(scores[b] - peak)
        scores[b] = w
        total += jnp.sum(w, axis=0, keepdims=True)
        acc += dot_nn(jnp.transpose(v_ref[b, 0]), w.astype(BF16))
    out_t = (acc / total).astype(BF16).astype(F32)
    o_ref[...] = jnp.transpose(out_t).astype(BF16)
    dsum = jnp.sum(jnp.transpose(g.astype(F32)) * out_t, axis=0, keepdims=True)
    inverse = 1.0 / total
    dq = jnp.zeros((HD, tok), F32)
    for b in range(blocks):
        probs = scores[b] * inverse
        dprobs = dot_nt(v_ref[b, 0], g)
        ds = (probs * (dprobs - dsum)).astype(BF16)
        dkv_ref[b, 0] = (dot_nn(ds, q) * scaling).astype(BF16)
        dkv_ref[b, 1] = dot_nn(probs.astype(BF16), g).astype(BF16)
        dq += dot_nn(jnp.transpose(k_ref[b, 0]), ds)
    dq_ref[...] = (jnp.transpose(dq) * scaling).astype(BF16)


def attention(qkv, grad, kv):
    tok, width = grad.shape
    heads, blocks = width // HD, kv.shape[0]
    one = pl.BlockSpec((tok, HD), lambda j: (0, j))
    return pl.pallas_call(
        functools.partial(attention_kernel, HD**-0.5),
        grid=(heads,),
        in_specs=[
            pl.BlockSpec((1, tok, HD), lambda j: (0, 0, j)),
            one,
            pl.BlockSpec((blocks, 1, tok, HD), lambda j: (0, 0, 0, j)),
            pl.BlockSpec((blocks, 1, tok, HD), lambda j: (0, 1, 0, j)),
        ],
        out_specs=[one, one, pl.BlockSpec((blocks, 2, tok, HD), lambda j: (0, 0, 0, j))],
        out_shape=[
            shaped((tok, width)),
            shaped((tok, width)),
            shaped((blocks, 2, tok, width)),
        ],
        scratch_shapes=[pltpu.VMEM((blocks, tok, tok), F32)],
        cost_estimate=cost(12 * tok * blocks * tok * width, 8 * 2**20, tok * blocks * tok * heads),
    )(qkv, grad, kv, kv)


def token_sum_kernel(place, *refs):
    own, other, xs, out, turned = refs[:4], refs[4:8], refs[8:12], refs[12], refs[13]
    i, c = pl.program_id(0), pl.program_id(1)
    tok = own[0].shape[1]

    for half, cols in enumerate((own, other)):

        @pl.when((c == 0) & (i == half))
        def _():
            for d in range(4):
                turned[:, d * tok : (d + 1) * tok] = jnp.transpose(cols[d][0])

    acc = dot_nn(turned[:, :tok], xs[0][0])
    for d in range(1, 4):
        acc += dot_nn(turned[:, d * tok : (d + 1) * tok], xs[d][0])
    acc = acc.astype(BF16)
    half = acc.shape[0] // 2

    @pl.when(place[5] == 0)
    def _():
        out[0, 0, 0] = acc[:half]
        out[0, 1, 0] = acc[half:]

    @pl.when(place[5] != 0)
    def _():
        out[0, 0, 0] = acc[half:]
        out[0, 1, 0] = acc[:half]


def token_sum(place, which, own, other, xs):
    _, tok, cols = own[0].shape
    kinds, _, width = xs[0].shape
    column = pl.BlockSpec((1, tok, cols), lambda i, c, s: (which, 0, 0))
    return pl.pallas_call(
        token_sum_kernel,
        grid_spec=pltpu.PrefetchScalarGridSpec(
            num_scalar_prefetch=1,
            grid=(2, kinds),
            in_specs=[column] * 8
            + [pl.BlockSpec((1, tok, width), lambda i, c, s: (c, 0, 0))] * 4,
            out_specs=pl.BlockSpec(
                (1, 2, 1, cols // 2, width), lambda i, c, s: (i ^ s[4], 0, c, 0, 0)
            ),
            scratch_shapes=[pltpu.VMEM((cols, 4 * tok), BF16)],
        ),
        out_shape=shaped((2, 2, kinds, cols // 2, width)),
        cost_estimate=cost(16 * tok * cols * kinds * width, 6 * 2**20),
    )(place, *own, *other, *xs)


def along_x(array):
    return [array] + [swap(array, "row_0", 4, d) for d in (1, 2, 3)]


def on_device(latent, hint, timestep, modulation, qkv_weight, out_weight, zero_weight, cotangent):
    tok, width = latent.shape
    x_pos, y_pos = lax.axis_index("row_0"), lax.axis_index("row_1")
    core_pos, group_pos = lax.axis_index("core"), lax.axis_index("group")
    head_pos = lax.axis_index("z") * 2 + core_pos
    control = group_pos == 0
    place = jnp.stack(
        [head_pos, core_pos, x_pos, group_pos, core_pos ^ group_pos, y_pos]
    ).astype(jnp.int32)
    w_qkv, w_out = qkv_weight[0], out_weight[0]
    full_width = w_out.shape[0]

    chosen = lax.dynamic_index_in_dim(modulation[0], timestep[0], 0, keepdims=False)
    mods_dev = lax.dynamic_slice_in_dim(chosen, head_pos * width, width, 1)
    scale_dev, gate_dev = mods_dev[1], mods_dev[2]

    summed = (latent.astype(F32) + hint.astype(F32)).astype(BF16)
    inputs = jnp.where(control, summed, latent)
    whole = gather_head(inputs)
    cot_late = lax.optimization_barrier((cotangent, whole[2], whole[4], whole[6]))[0]
    cot_full = gather_head(cot_late)
    ncols, qkv, stats = norm_qkv(place, whole, chosen, w_qkv)
    kv_full = lax.all_to_all(
        jnp.broadcast_to(qkv[1:], (8, 2, tok, width)), ROW, split_axis=0, concat_axis=0, tiled=True
    )

    incoming, gated, ccols = hint_back(place, cot_full, chosen, zero_weight)
    gated_full = gather_head(gated)
    attn_grad, *packs = branch_grad(place, gated_full, w_out, ncols, ccols)
    cols = packs[:1] + [swap(packs[d], "row_0", 4, d) for d in (1, 2, 3)]
    cols_other = [swap(a, "core", 2, 1) for a in cols]

    attn, dquery, dkv = attention(qkv, attn_grad, kv_full)
    dkv_all = lax.all_to_all(dkv, ROW, split_axis=0, concat_axis=0, tiled=True)

    branch = sum_head(*spread(place, attn, w_out))
    state = (inputs.astype(F32) + gate_dev * branch).astype(BF16)
    other_state = swap(state, "group", 2, 1)
    control_out = jnp.where(control, state, other_state)
    main_out = jnp.where(control, other_state, state)
    zero_own, zero_other = spread(place, control_out, zero_weight)

    dkv_all, zero_own = lax.optimization_barrier((dkv_all, zero_own))
    dkv_sum = jnp.sum(dkv_all.astype(F32), axis=0).astype(BF16)
    grads = jnp.concatenate([dquery[None], dkv_sum])
    grads_x = along_x(grads)
    projected = sum_head(zero_own, zero_other)
    mixed = (main_out.astype(F32) + projected).astype(BF16)
    own_terms, other_terms, sums = spread_norm(place, grads, w_qkv, chosen, stats, whole)
    for axis, size, d in (("core", 2, 1), ("z", 4, 1), ("z", 4, 2)):
        sums = sums + swap(sums, axis, size, d)
    dnorm = sum_head(own_terms, other_terms)
    mean, rstd = stats[0, :, :1], stats[1, :, :1]
    nhat_dev = (inputs.astype(F32) - mean) * rstd
    first = sums[0][:, None] / full_width
    second = sums[1][:, None] / full_width
    d_in = incoming.astype(F32) + rstd * (dnorm * (1.0 + scale_dev) - first - nhat_dev * second)
    half = tok // 2
    own_half = lax.dynamic_slice_in_dim(d_in, group_pos * half, half, 0)
    sent_half = lax.dynamic_slice_in_dim(d_in, (1 - group_pos) * half, half, 0)
    other_half = swap(sent_half, "group", 2, 1)
    latent_grad = (own_half + other_half)[None, None]
    hint_grad = jnp.where(control, own_half, other_half)[None, None]

    attn_or_state = jnp.where(control, attn, control_out)
    side = token_sum(place, 1, cols, cols_other, along_x(attn_or_state[None]))
    near = side[0, 0, 0].astype(F32) + swap(side[0, 1, 0], "row_1", 2, 1).astype(F32)
    far = swap(side[1, 0, 0], "group", 2, 1).astype(F32) + moved(
        side[1, 1, 0], YAX, [(0, 3), (1, 2), (2, 1), (3, 0)]
    ).astype(F32)
    out_grad = jnp.where(control, near, far)
    zero_grad = jnp.where(control, far, near)

    main = token_sum(place, 0, cols, cols_other, grads_x)
    near = main[0, 0].astype(F32) + moved(main[0, 1], YAX, [(0, 1), (1, 0)]).astype(F32)
    far = moved(main[1, 0], YAX, [(0, 2), (1, 3)]).astype(F32) + moved(
        main[1, 1], YAX, [(0, 3), (1, 2)]
    ).astype(F32)
    qkv_grad = jnp.where(control, near, far).transpose(1, 0, 2)
    return (mixed, latent_grad, hint_grad, qkv_grad, out_grad, zero_grad)


def solution(mesh):
    torus = Mesh(
        mesh.devices.reshape(mesh.shape["group"], 4, 2, 4, 2),
        ("group", "row_0", "row_1", "z", "core"),
    )

    return jax.shard_map(
        on_device,
        mesh=torus,
        in_specs=(
            P(ROW, HEAD),
            P(ROW, HEAD),
            P(),
            P("group", None, None, None),
            P("group", None, None, HEAD),
            P("group", None, HEAD),
            P(None, HEAD),
            P(ROW, HEAD),
        ),
        out_specs=(
            P(ROW, HEAD),
            P(ROW, "group", None, HEAD),
            P(ROW, "group", None, HEAD),
            P(GROUP_ROW, None, HEAD),
            P(GROUP_ROW, HEAD),
            P(GROUP_ROW, HEAD),
        ),
        check_vma=False,
    )
```

```python
import functools

import jax
import jax.numpy as jnp
from jax import lax
from jax.experimental import pallas as pl
from jax.experimental.pallas import tpu as pltpu
from jax.sharding import Mesh
from jax.sharding import PartitionSpec as P


HD = 128
ROW = ("row_0", "row_1")
HEAD = ("z", "core")
GROUP_ROW = ("group", "row_0", "row_1")
YAX = ("group", "row_1")
EPS = 1e-06
F32 = jnp.float32
BF16 = jnp.bfloat16
ANY = pl.BlockSpec(memory_space=pl.ANY)


def dot_nn(a, b):
    return lax.dot_general(a, b, (((1,), (0,)), ((), ())), preferred_element_type=F32)


def dot_nt(a, b):
    return lax.dot_general(a, b, (((1,), (1,)), ((), ())), preferred_element_type=F32)


def moved(array, axis, pairs):
    return lax.ppermute(array, axis, pairs)


def swap(array, axis, size, distance):
    return moved(array, axis, [(i, i ^ distance) for i in range(size)])


def cost(flops, size, trans=0):
    return pl.CostEstimate(flops=flops, bytes_accessed=size, transcendentals=trans)


def shaped(shape, dtype=BF16):
    return jax.ShapeDtypeStruct(shape, dtype)


def full(shape):
    return pl.BlockSpec(shape, lambda *a: (0,) * len(shape))


def run(body, place, args, specs, outs, scratch, estimate):
    return pl.pallas_call(
        body,
        grid_spec=pltpu.PrefetchScalarGridSpec(
            num_scalar_prefetch=1,
            grid=(1,),
            in_specs=specs,
            out_specs=[full(o.shape) for o in outs],
            scratch_shapes=scratch,
        ),
        out_shape=outs,
        cost_estimate=estimate,
    )(place, *args)


def gather_head(own):
    mine = [own] + [swap(own, "z", 4, d) for d in (1, 2, 3)]
    pieces = []
    for a in mine:
        pieces += [a, swap(a, "core", 2, 1)]
    return pieces


def sum_head(own, other):
    got = swap(other, "core", 2, 1)
    sums = [own[d].astype(F32) + got[d].astype(F32) for d in range(4)]
    total = sums[0]
    for d in (1, 2, 3):
        total = total + swap(sums[d].astype(BF16), "z", 4, d).astype(F32)
    return total


def lanes(index, width):
    return pl.ds(pl.multiple_of(index * width, 128), width)


def lay_out(place, pieces, whole):
    width = pieces[0].shape[1]
    for p, piece in enumerate(pieces):
        whole[:, lanes(place[0] ^ p, width)] = piece[...]


def norm_qkv_kernel(place, *refs):
    pieces, (mods, w) = refs[:8], refs[8:10]
    cols, q_out, kv_out, stats = refs[10:14]
    whole, wbuf, sems = refs[14:]
    tok, width = pieces[0].shape

    def fetch(c):
        return pltpu.make_async_copy(w.at[c], wbuf.at[c], sems.at[c])

    for c in range(3):
        fetch(c).start()
    lay_out(place, pieces, whole)
    features = 8 * width
    zero = jnp.zeros((tok, 1), F32)

    def chunk(k):
        return whole[:, lanes(k, width)].astype(F32)

    mean = lax.fori_loop(
        0, 8, lambda k, t: t + jnp.sum(chunk(k), axis=-1, keepdims=True), zero, unroll=2
    ) / features

    def squares(k, t):
        c = chunk(k) - mean
        return t + jnp.sum(c * c, axis=-1, keepdims=True)

    rstd = lax.rsqrt(lax.fori_loop(0, 8, squares, zero, unroll=2) / features + EPS)
    stats[0] = jnp.broadcast_to(mean, stats.shape[1:])
    stats[1] = jnp.broadcast_to(rstd, stats.shape[1:])

    @pl.loop(0, 8, unroll=2)
    def _(k):
        at = lanes(k, width)
        nhat = (chunk(k) - mean) * rstd
        n = (nhat * (1.0 + mods[1:2, at]) + mods[0:1, at]).astype(BF16)
        whole[:, at] = n

        @pl.when(place[1] == k // 4)
        def _():
            cols[place[2] ^ (k % 4)] = n

    @pl.loop(0, 3)
    def _(c):
        fetch(c).wait()
        part = dot_nn(whole[...], wbuf[c]).astype(BF16)

        @pl.when(c == 0)
        def _():
            q_out[...] = part

        @pl.when(c > 0)
        def _():
            kv_out[jnp.maximum(c - 1, 0)] = part


def norm_qkv(place, pieces, mods, w):
    tok, width = pieces[0].shape
    return run(
        norm_qkv_kernel,
        place,
        (*pieces, mods, w),
        [full((tok, width))] * 8 + [full(mods.shape), ANY],
        [
            shaped((4, tok, width)),
            shaped((tok, width)),
            shaped((2, tok, width)),
            shaped((2, tok, 128), F32),
        ],
        [
            pltpu.VMEM((tok, 8 * width), BF16),
            pltpu.VMEM(w.shape, BF16),
            pltpu.SemaphoreType.DMA((3,)),
        ],
        cost(2 * tok * 8 * width * 3 * width, 12 * 2**20),
    )


def hint_kernel(place, *refs):
    pieces, (mods, w) = refs[:8], refs[8:10]
    incoming, gated, cols = refs[10:13]
    whole, wbuf, sem = refs[13:]
    width = pieces[0].shape[1]
    copy = pltpu.make_async_copy(w, wbuf, sem.at[0])
    copy.start()
    lay_out(place, pieces, whole)
    for d in range(4):
        cols[d] = whole[:, lanes(place[1] * 4 + (place[2] ^ d), width)]
    copy.wait()
    back = dot_nn(whole[...], wbuf[...]).astype(BF16)
    got = jnp.where(place[3] == 0, back, pieces[0][...])
    incoming[...] = got
    gate = mods[2:3, lanes(place[0], width)]
    gated[...] = (gate * got.astype(F32)).astype(BF16)


def hint_back(place, pieces, mods, w):
    tok, width = pieces[0].shape
    return run(
        hint_kernel,
        place,
        (*pieces, mods, w),
        [full((tok, width))] * 8 + [full(mods.shape), ANY],
        [shaped((tok, width)), shaped((tok, width)), shaped((4, tok, width))],
        [
            pltpu.VMEM((tok, 8 * width), BF16),
            pltpu.VMEM(w.shape, BF16),
            pltpu.SemaphoreType.DMA((1,)),
        ],
        cost(2 * tok * 8 * width * width, 6 * 2**20),
    )


def branch_grad_kernel(place, *refs):
    pieces, (w, ncols, ccols) = refs[:8], refs[8:11]
    out, packs = refs[11], refs[12:16]
    whole, wbuf, sem = refs[16:]
    width = pieces[0].shape[1]
    copy = pltpu.make_async_copy(w, wbuf, sem.at[0])
    copy.start()
    lay_out(place, pieces, whole)
    for d in range(4):
        packs[d][0] = ncols[d]

        @pl.when(place[3] == 0)
        def _():
            packs[d][1] = whole[:, lanes(place[1] * 4 + (place[2] ^ d), width)]

        @pl.when(place[3] != 0)
        def _():
            packs[d][1] = ccols[d]

    copy.wait()
    out[...] = dot_nn(whole[...], wbuf[...]).astype(BF16)


def branch_grad(place, pieces, w, ncols, ccols):
    tok, width = pieces[0].shape
    return run(
        branch_grad_kernel,
        place,
        (*pieces, w, ncols, ccols),
        [full((tok, width))] * 8 + [ANY, full(ncols.shape), full(ccols.shape)],
        [shaped((tok, width))] + [shaped((2, tok, width))] * 4,
        [
            pltpu.VMEM((tok, 8 * width), BF16),
            pltpu.VMEM(w.shape, BF16),
            pltpu.SemaphoreType.DMA((1,)),
        ],
        cost(2 * tok * 8 * width * width, 8 * 2**20),
    )


def spread_kernel(place, a, w, own, other, wbuf, sems):
    width = a.shape[1]
    pair = 2 * width
    copies = []
    for d in range(4):
        rows = pl.ds(pl.multiple_of(((place[0] // 2) ^ d) * pair, pair), pair)
        copies.append(pltpu.make_async_copy(w.at[rows], wbuf.at[d], sems.at[d]))
        copies[-1].start()
    for d in range(4):
        copies[d].wait()
        part = dot_nt(a[...], wbuf[d]).astype(BF16)

        @pl.when(place[1] == 0)
        def _():
            own[d] = part[:, :width]
            other[d] = part[:, width:]

        @pl.when(place[1] != 0)
        def _():
            own[d] = part[:, width:]
            other[d] = part[:, :width]


def spread(place, a, w):
    tok, width = a.shape
    return run(
        spread_kernel,
        place,
        (a, w),
        [full((tok, width)), ANY],
        [shaped((4, tok, width))] * 2,
        [pltpu.VMEM((4, 2 * width, width), BF16), pltpu.SemaphoreType.DMA((4,))],
        cost(2 * tok * 8 * width * width, 6 * 2**20),
    )


def spread_norm_kernel(place, grads, w, mods, stats, *refs):
    pieces, (own, other, sums, whole, wbuf, sems) = refs[:8], refs[8:]
    tok, width = pieces[0].shape
    pair = 2 * width

    def fetch(d):
        rows = pl.ds(pl.multiple_of(((place[0] // 2) ^ d) * pair, pair), pair)
        return pltpu.make_async_copy(w.at[:, rows], wbuf.at[d], sems.at[d])

    for d in range(4):
        fetch(d).start()
    lay_out(place, pieces, whole)
    mean, rstd = stats[0, :, :1], stats[1, :, :1]
    zero = jnp.zeros((tok, 1), F32)

    def step(d, totals):
        first, second = totals
        fetch(d).wait()
        part = (
            dot_nt(grads[0], wbuf[d, 0])
            + dot_nt(grads[1], wbuf[d, 1])
            + dot_nt(grads[2], wbuf[d, 2])
        )
        low, high = part[:, :width].astype(BF16), part[:, width:].astype(BF16)

        @pl.when(place[1] == 0)
        def _():
            own[d] = low
            other[d] = high

        @pl.when(place[1] != 0)
        def _():
            own[d] = high
            other[d] = low

        at = lanes((place[0] // 2) ^ d, pair)
        scaled = part * (1.0 + mods[1:2, at])
        nhat = (whole[:, at].astype(F32) - mean) * rstd
        first += jnp.sum(scaled, axis=-1, keepdims=True)
        second += jnp.sum(scaled * nhat, axis=-1, keepdims=True)
        return first, second

    first, second = lax.fori_loop(0, 4, step, (zero, zero))
    lane = lax.broadcasted_iota(jnp.int32, (tok, 128), 1)
    both = jnp.where(lane == 0, first, jnp.where(lane == 1, second, 0.0))
    sums[...] = jnp.transpose(both)[:8]


def spread_norm(place, grads, w, mods, stats, pieces):
    _, tok, width = grads.shape
    return run(
        spread_norm_kernel,
        place,
        (grads, w, mods, stats, *pieces),
        [full(grads.shape), ANY, full(mods.shape), full(stats.shape)]
        + [full((tok, width))] * 8,
        [shaped((4, tok, width))] * 2 + [shaped((8, tok), F32)],
        [
            pltpu.VMEM((tok, 8 * width), BF16),
            pltpu.VMEM((4, 3, 2 * width, width), BF16),
            pltpu.SemaphoreType.DMA((4,)),
        ],
        cost(6 * tok * 8 * width * width, 14 * 2**20),
    )


def attention_kernel(scaling, q_ref, g_ref, k_ref, v_ref, o_ref, dq_ref, dkv_ref, scores):
    q, g = q_ref[...], g_ref[...]
    blocks, _, tok, _ = k_ref.shape
    peak = None
    for b in range(blocks):
        s = dot_nt(k_ref[b, 0], q) * scaling
        scores[b] = s
        top = jnp.max(s, axis=0, keepdims=True)
        peak = top if peak is None else jnp.maximum(peak, top)
    total = jnp.zeros((1, tok), F32)
    acc = jnp.zeros((HD, tok), F32)
    for b in range(blocks):
        w = jnp.exp(scores[b] - peak)
        scores[b] = w
        total += jnp.sum(w, axis=0, keepdims=True)
        acc += dot_nn(jnp.transpose(v_ref[b, 0]), w.astype(BF16))
    out_t = (acc / total).astype(BF16).astype(F32)
    o_ref[...] = jnp.transpose(out_t).astype(BF16)
    dsum = jnp.sum(jnp.transpose(g.astype(F32)) * out_t, axis=0, keepdims=True)
    inverse = 1.0 / total
    dq = jnp.zeros((HD, tok), F32)
    for b in range(blocks):
        probs = scores[b] * inverse
        dprobs = dot_nt(v_ref[b, 0], g)
        ds = (probs * (dprobs - dsum)).astype(BF16)
        dkv_ref[b, 0] = (dot_nn(ds, q) * scaling).astype(BF16)
        dkv_ref[b, 1] = dot_nn(probs.astype(BF16), g).astype(BF16)
        dq += dot_nn(jnp.transpose(k_ref[b, 0]), ds)
    dq_ref[...] = (jnp.transpose(dq) * scaling).astype(BF16)


def attention(query, grad, kv):
    tok, width = grad.shape
    heads, blocks = width // HD, kv.shape[0]
    one = pl.BlockSpec((tok, HD), lambda j: (0, j))
    return pl.pallas_call(
        functools.partial(attention_kernel, HD**-0.5),
        grid=(heads,),
        in_specs=[
            one,
            one,
            pl.BlockSpec((blocks, 1, tok, HD), lambda j: (0, 0, 0, j)),
            pl.BlockSpec((blocks, 1, tok, HD), lambda j: (0, 1, 0, j)),
        ],
        out_specs=[one, one, pl.BlockSpec((blocks, 2, tok, HD), lambda j: (0, 0, 0, j))],
        out_shape=[
            shaped((tok, width)),
            shaped((tok, width)),
            shaped((blocks, 2, tok, width)),
        ],
        scratch_shapes=[pltpu.VMEM((blocks, tok, tok), F32)],
        cost_estimate=cost(12 * tok * blocks * tok * width, 8 * 2**20, tok * blocks * tok * heads),
    )(query, grad, kv, kv)


def token_sum_kernel(place, *refs):
    own, other, xs, out, turned = refs[:4], refs[4:8], refs[8:12], refs[12], refs[13]
    i, c = pl.program_id(0), pl.program_id(1)
    tok = own[0].shape[1]

    for half, cols in enumerate((own, other)):

        @pl.when((c == 0) & (i == half))
        def _():
            for d in range(4):
                turned[:, d * tok : (d + 1) * tok] = jnp.transpose(cols[d][0])

    acc = dot_nn(turned[:, :tok], xs[0][0])
    for d in range(1, 4):
        acc += dot_nn(turned[:, d * tok : (d + 1) * tok], xs[d][0])
    acc = acc.astype(BF16)
    half = acc.shape[0] // 2

    @pl.when(place[5] == 0)
    def _():
        out[0, 0, 0] = acc[:half]
        out[0, 1, 0] = acc[half:]

    @pl.when(place[5] != 0)
    def _():
        out[0, 0, 0] = acc[half:]
        out[0, 1, 0] = acc[:half]


def token_sum(place, which, own, other, xs):
    _, tok, cols = own[0].shape
    kinds, _, width = xs[0].shape
    column = pl.BlockSpec((1, tok, cols), lambda i, c, s: (which, 0, 0))
    return pl.pallas_call(
        token_sum_kernel,
        grid_spec=pltpu.PrefetchScalarGridSpec(
            num_scalar_prefetch=1,
            grid=(2, kinds),
            in_specs=[column] * 8
            + [pl.BlockSpec((1, tok, width), lambda i, c, s: (c, 0, 0))] * 4,
            out_specs=pl.BlockSpec(
                (1, 2, 1, cols // 2, width), lambda i, c, s: (i ^ s[4], 0, c, 0, 0)
            ),
            scratch_shapes=[pltpu.VMEM((cols, 4 * tok), BF16)],
        ),
        out_shape=shaped((2, 2, kinds, cols // 2, width)),
        cost_estimate=cost(16 * tok * cols * kinds * width, 6 * 2**20),
    )(place, *own, *other, *xs)


def along_x(array):
    return [array] + [swap(array, "row_0", 4, d) for d in (1, 2, 3)]


def on_device(latent, hint, timestep, modulation, qkv_weight, out_weight, zero_weight, cotangent):
    tok, width = latent.shape
    x_pos, y_pos = lax.axis_index("row_0"), lax.axis_index("row_1")
    core_pos, group_pos = lax.axis_index("core"), lax.axis_index("group")
    head_pos = lax.axis_index("z") * 2 + core_pos
    control = group_pos == 0
    place = jnp.stack(
        [head_pos, core_pos, x_pos, group_pos, core_pos ^ group_pos, y_pos]
    ).astype(jnp.int32)
    w_qkv, w_out = qkv_weight[0], out_weight[0]
    full_width = w_out.shape[0]

    chosen = lax.dynamic_index_in_dim(modulation[0], timestep[0], 0, keepdims=False)
    mods_dev = lax.dynamic_slice_in_dim(chosen, head_pos * width, width, 1)
    scale_dev, gate_dev = mods_dev[1], mods_dev[2]

    summed = (latent.astype(F32) + hint.astype(F32)).astype(BF16)
    inputs = jnp.where(control, summed, latent)
    whole = gather_head(inputs)
    cot_late = lax.optimization_barrier((cotangent, whole[2], whole[4], whole[6]))[0]
    cot_full = gather_head(cot_late)
    ncols, query, kv, stats = norm_qkv(place, whole, chosen, w_qkv)
    kv_full = lax.all_to_all(
        jnp.broadcast_to(kv, (8, *kv.shape)), ROW, split_axis=0, concat_axis=0, tiled=True
    )

    incoming, gated, ccols = hint_back(place, cot_full, chosen, zero_weight)
    gated_full = gather_head(gated)
    attn_grad, *packs = branch_grad(place, gated_full, w_out, ncols, ccols)
    cols = packs[:1] + [swap(packs[d], "row_0", 4, d) for d in (1, 2, 3)]
    cols_other = [swap(a, "core", 2, 1) for a in cols]

    attn, dquery, dkv = attention(query, attn_grad, kv_full)
    dkv_all = lax.all_to_all(dkv, ROW, split_axis=0, concat_axis=0, tiled=True)

    branch = sum_head(*spread(place, attn, w_out))
    state = (inputs.astype(F32) + gate_dev * branch).astype(BF16)
    other_state = swap(state, "group", 2, 1)
    control_out = jnp.where(control, state, other_state)
    main_out = jnp.where(control, other_state, state)
    zero_own, zero_other = spread(place, control_out, zero_weight)

    dkv_all, zero_own = lax.optimization_barrier((dkv_all, zero_own))
    dkv_sum = jnp.sum(dkv_all.astype(F32), axis=0).astype(BF16)
    grads = jnp.concatenate([dquery[None], dkv_sum])
    grads_x = along_x(grads)
    projected = sum_head(zero_own, zero_other)
    mixed = (main_out.astype(F32) + projected).astype(BF16)
    own_terms, other_terms, sums = spread_norm(place, grads, w_qkv, chosen, stats, whole)
    for axis, size, d in (("core", 2, 1), ("z", 4, 1), ("z", 4, 2)):
        sums = sums + swap(sums, axis, size, d)
    dnorm = sum_head(own_terms, other_terms)
    mean, rstd = stats[0, :, :1], stats[1, :, :1]
    nhat_dev = (inputs.astype(F32) - mean) * rstd
    first = sums[0][:, None] / full_width
    second = sums[1][:, None] / full_width
    d_in = incoming.astype(F32) + rstd * (dnorm * (1.0 + scale_dev) - first - nhat_dev * second)
    half = tok // 2
    own_half = lax.dynamic_slice_in_dim(d_in, group_pos * half, half, 0)
    sent_half = lax.dynamic_slice_in_dim(d_in, (1 - group_pos) * half, half, 0)
    other_half = swap(sent_half, "group", 2, 1)
    latent_grad = (own_half + other_half)[None, None]
    hint_grad = jnp.where(control, own_half, other_half)[None, None]

    attn_or_state = jnp.where(control, attn, control_out)
    side = token_sum(place, 1, cols, cols_other, along_x(attn_or_state[None]))
    near = side[0, 0, 0].astype(F32) + swap(side[0, 1, 0], "row_1", 2, 1).astype(F32)
    far = swap(side[1, 0, 0], "group", 2, 1).astype(F32) + moved(
        side[1, 1, 0], YAX, [(0, 3), (1, 2), (2, 1), (3, 0)]
    ).astype(F32)
    out_grad = jnp.where(control, near, far)
    zero_grad = jnp.where(control, far, near)

    main = token_sum(place, 0, cols, cols_other, grads_x)
    near = main[0, 0].astype(F32) + moved(main[0, 1], YAX, [(0, 1), (1, 0)]).astype(F32)
    far = moved(main[1, 0], YAX, [(0, 2), (1, 3)]).astype(F32) + moved(
        main[1, 1], YAX, [(0, 3), (1, 2)]
    ).astype(F32)
    qkv_grad = jnp.where(control, near, far).transpose(1, 0, 2)
    return (mixed, latent_grad, hint_grad, qkv_grad, out_grad, zero_grad)


def solution(mesh):
    torus = Mesh(
        mesh.devices.reshape(mesh.shape["group"], 4, 2, 4, 2),
        ("group", "row_0", "row_1", "z", "core"),
    )

    return jax.shard_map(
        on_device,
        mesh=torus,
        in_specs=(
            P(ROW, HEAD),
            P(ROW, HEAD),
            P(),
            P("group", None, None, None),
            P("group", None, None, HEAD),
            P("group", None, HEAD),
            P(None, HEAD),
            P(ROW, HEAD),
        ),
        out_specs=(
            P(ROW, HEAD),
            P(ROW, "group", None, HEAD),
            P(ROW, "group", None, HEAD),
            P(GROUP_ROW, None, HEAD),
            P(GROUP_ROW, HEAD),
            P(GROUP_ROW, HEAD),
        ),
        check_vma=False,
    )
```
